32 devices in a mesh: sweep: 2 (over x), cx: 4 (over z), cy: 4 (over y, core).
Axes of the slice: x: 2, y: 2, z: 4, core: 2. Of those that a mesh axis runs over, the one named last changes fastest.
Arguments:
- right_side: float32 [2, 320, 32, 512], P('sweep', None, 'cx', 'cy'), may hold values from -6 to 6
- inverse_table: bfloat16 [4, 320, 320], replicated, may hold values from -1 to 3
- coupling_table: bfloat16 [2, 6, 80, 320], replicated, may hold values from -0.3125 to 0.3125
- block_kind: int32 [2, 32, 512], P('sweep', 'cx', 'cy'), may hold values from 0 to 3
- face_kind: int32 [2, 6, 32, 512], P('sweep', None, 'cx', 'cy'), may hold values from 0 to 1
Outputs:
- solution: float32 [2, 320, 32, 512], P('sweep', None, 'cx', 'cy')
The draws below stay inside these ranges and needn't reach their ends.
All inputs are finite; a program needn't handle non-finite values.
Results may differ from the reference program's by a relative error of at most 0.0095.
Values may be sent and summed in bfloat16 or wider, within the bound.
A program may use at most 64 MiB of HBM per device.

```python
import math
import jax
import jax.numpy as jnp
from jax import lax

NVAR = 5
NP = 4
BLOCK = 320
TRACE = 80
KD = 4
KC = 2
SWEEPS = 2
NS = 2
NX = 32
NY = 512


def draw_inverse_table(key, part):
    first_key, second_key = jax.random.split(key)
    index_row = jnp.arange(BLOCK)
    identity = (index_row[:, None] == index_row[None, :]).astype(jnp.float32)
    diagonal = jax.random.uniform(first_key, (KD, BLOCK, 1), jnp.float32, 0.5, 1.5)
    spread = jax.random.truncated_normal(second_key, -4.0, 4.0, (KD, BLOCK, BLOCK), jnp.float32) * (0.3 / math.sqrt(BLOCK))
    return (identity * diagonal + (1.0 - identity) * spread).astype(jnp.bfloat16)


def with_ends(array, own_key, low, high):
    longest = array.shape.index(max(array.shape))
    spots = []
    for shift in (0, 1):
        where = [jax.random.randint(jax.random.fold_in(own_key, axis), (), 0, length) for axis, length in enumerate(array.shape)]
        where[longest] = (where[longest] + shift) % array.shape[longest]
        spots.append(tuple(where))
    return array.at[spots[0]].set(low).at[spots[1]].set(high)


def steps_of(stream_key, dims, pieces, low, top_value):
    def one(position, blocks):
        draws = jax.random.uniform(jax.random.fold_in(jax.random.fold_in(stream_key, 6), position), (blocks,), jnp.float32, low / len(pieces), top_value / len(pieces))
        return jnp.repeat(jnp.exp(draws), dims[position] // blocks).reshape((-1,) + (1,) * (len(dims) - position - 1))

    factor_of = one(*pieces[0])
    for cut in pieces[1:]:
        factor_of = factor_of * one(*cut)
    return factor_of


def bell_draw(key, extent, width, most, cuts=(), kind=jnp.bfloat16):
    drawn = width * jax.random.normal(key, extent, jnp.float32)
    if cuts:
        drawn = drawn * steps_of(key, extent, cuts, -0.22, 0.18)
    return jnp.clip(drawn, -most, most).astype(kind)


def setup_inputs(seed: int = 0) -> dict:
    key_list = jax.random.split(jax.random.key(seed), 6)
    return {
        "right_side": bell_draw(key_list[0], (NS, BLOCK, NX, NY), 1.0, 6.0, ((0, 2), (2, 4), (3, 4)), jnp.float32),
        "inverse_table": draw_inverse_table(jax.random.fold_in(key_list[5], 71), 0),
        "coupling_table": bell_draw(key_list[2], (KC, 6, TRACE, BLOCK), (4 * TRACE) ** -0.5, 0.3125),
        "block_kind": with_ends(jax.random.randint(key_list[3], (NS, NX, NY), 0, KD), jax.random.fold_in(key_list[3], 1), 0, KD - 1).astype(jnp.int32),
        "face_kind": with_ends(jax.random.randint(key_list[4], (NS, 6, NX, NY), 0, KC), jax.random.fold_in(key_list[4], 1), 0, KC - 1).astype(jnp.int32),
    }


def face_traces(iterate):
    plane_count, _, width_x, width_y = iterate.shape
    node_view = iterate.reshape(plane_count, NVAR, NP, NP, NP, width_x, width_y)
    picked = (node_view[:, :, 0], node_view[:, :, NP - 1], node_view[:, :, :, 0], node_view[:, :, :, NP - 1], node_view[:, :, :, :, 0], node_view[:, :, :, :, NP - 1])
    return [member.reshape(plane_count, TRACE, width_x, width_y).astype(jnp.bfloat16) for member in picked]


def from_below(source, along_dim):
    length = source.shape[along_dim]
    zero_row = jnp.zeros_like(lax.slice_in_dim(source, 0, 1, axis=along_dim))
    return jnp.concatenate([zero_row, lax.slice_in_dim(source, 0, length - 1, axis=along_dim)], axis=along_dim)


def from_above(source, along_dim):
    length = source.shape[along_dim]
    zero_row = jnp.zeros_like(lax.slice_in_dim(source, 0, 1, axis=along_dim))
    return jnp.concatenate([lax.slice_in_dim(source, 1, length, axis=along_dim), zero_row], axis=along_dim)


def couple_terms(incoming, kinds_plane, coupling_table):
    accumulated = jnp.zeros((BLOCK,) + incoming[0].shape[1:], jnp.float32)
    for face_index in range(6):
        for kind_index in range(KC):
            masked = jnp.where(kinds_plane[face_index] == kind_index, incoming[face_index], jnp.zeros_like(incoming[face_index]))
            accumulated = accumulated + jnp.einsum("ji,jxy->ixy", coupling_table[kind_index, face_index].astype(jnp.float32), masked.astype(jnp.float32), precision=lax.Precision.HIGHEST)
    return accumulated


def apply_inverse(residual, kinds_plane, inverse_table):
    result = jnp.zeros(residual.shape, jnp.float32)
    for kind_index in range(KD):
        masked = jnp.where(kinds_plane[None] == kind_index, residual, jnp.zeros_like(residual))
        result = result + jnp.einsum("ij,jxy->ixy", inverse_table[kind_index].astype(jnp.float32), masked.astype(jnp.float32), precision=lax.Precision.HIGHEST)
    return result


def half_sweep(iterate, right_side, inverse_table, coupling_table, block_kind, face_kind, forward):
    sweep_low, sweep_high, low_x, high_x, low_y, high_y = face_traces(iterate)
    from_xlow = from_below(high_x, 2)
    from_xhigh = from_above(low_x, 2)
    from_ylow = from_below(high_y, 3)
    from_yhigh = from_above(low_y, 3)
    if forward:
        other_side = from_above(sweep_low, 0)
    else:
        other_side = from_below(sweep_high, 0)
    width_x = iterate.shape[2]
    width_y = iterate.shape[3]

    def advance(front_trace, inputs):
        rhs_plane, kinds_plane, faces_plane, other_plane, xlow_plane, xhigh_plane, ylow_plane, yhigh_plane = inputs
        if forward:
            incoming = [front_trace, other_plane, xlow_plane, xhigh_plane, ylow_plane, yhigh_plane]
        else:
            incoming = [other_plane, front_trace, xlow_plane, xhigh_plane, ylow_plane, yhigh_plane]
        residual = (rhs_plane - couple_terms(incoming, faces_plane, coupling_table)).astype(jnp.bfloat16)
        updated = apply_inverse(residual, kinds_plane, inverse_table)
        node_view = updated.reshape(NVAR, NP, NP * NP, width_x, width_y)
        picked = node_view[:, NP - 1] if forward else node_view[:, 0]
        return picked.reshape(TRACE, width_x, width_y).astype(jnp.bfloat16), updated

    start_trace = jnp.zeros((TRACE, width_x, width_y), jnp.bfloat16)
    _, plane_stack = lax.scan(advance, start_trace, (right_side, block_kind, face_kind, other_side, from_xlow, from_xhigh, from_ylow, from_yhigh), reverse=not forward)
    return plane_stack


def reference(right_side, inverse_table, coupling_table, block_kind, face_kind):
    iterate = jnp.zeros(right_side.shape, jnp.float32)
    for sweep_index in range(SWEEPS):
        iterate = half_sweep(iterate, right_side, inverse_table, coupling_table, block_kind, face_kind, True)
        iterate = half_sweep(iterate, right_side, inverse_table, coupling_table, block_kind, face_kind, False)
    return iterate
```

```python
import functools
import jax
import jax.numpy as jnp
from jax import lax
from jax.experimental import pallas as pl
from jax.experimental.pallas import tpu as pltpu
from jax.sharding import PartitionSpec as P

NVAR = 5
NP = 4
BLOCK = 320
TRACE = 80
KD = 4
KC = 2
SWEEPS = 2
HALVES = 2 * SWEEPS
LANES = 128
WIDE = 256
REST = BLOCK - WIDE
GROUP = 2
COLS = GROUP * LANES
DEPTH = KD * BLOCK
LATERAL = 4 * TRACE
PACK = 16
MESH = pl.DeviceIdType.MESH
F32 = jnp.float32
BF16 = jnp.bfloat16


def kernel(
    rows,
    rhs_hbm,
    table_hbm,
    coupling_hbm,
    kind_hbm,
    face_hbm,
    out_ref,
    rhs_ref,
    table_ref,
    coupling_ref,
    kind_ref,
    face_ref,
    full_ref,
    trace_ref,
    tall_ref,
    lat_ref,
    chain_ref,
    kmask_ref,
    fmask_ref,
    base_ref,
    prod_ref,
    lat_stack,
    chain_stack,
    inv_stack,
    front_in,
    front_out,
    x_low,
    x_high,
    y_own,
    y_in,
    y_out,
    load_sem,
    front_send,
    front_recv,
    x_send,
    x_recv,
    y_send,
    y_recv,
):
    groups = rows // GROUP
    places = {}
    for name in ("sweep", "cx", "cy"):
        places[name] = (lax.axis_index(name), lax.axis_size(name))

    def has(name, step):
        spot, count = places[name]
        return spot < count - 1 if step > 0 else spot > 0

    def partner(name, step):
        return {name: places[name][0] + step}

    for half in range(HALVES - 1):
        x_high[half, 0] = jnp.zeros((TRACE, LANES), BF16)
        x_low[half, rows + 1] = jnp.zeros((TRACE, LANES), BF16)
    for side in range(2):

        @pl.when(jnp.logical_not(has("cy", 2 * side - 1)))
        def _():
            for half in range(HALVES - 1):
                y_in[half, side] = jnp.zeros((groups, TRACE, LANES), BF16)

    barrier = pltpu.get_barrier_semaphore()
    total = 0
    for name in ("sweep", "cx", "cy"):
        for step in (-1, 1):
            exists = has(name, step)
            total = total + jnp.where(exists, 1, 0)

            @pl.when(exists)
            def _():
                pl.semaphore_signal(
                    barrier, inc=1, device_id=partner(name, step), device_id_type=MESH
                )

    loads = [
        pltpu.make_async_copy(table_hbm, table_ref, load_sem.at[0]),
        pltpu.make_async_copy(kind_hbm, kind_ref, load_sem.at[1]),
        pltpu.make_async_copy(face_hbm, face_ref, load_sem.at[2]),
        pltpu.make_async_copy(coupling_hbm, coupling_ref, load_sem.at[3]),
    ]
    for row in range(rows):
        loads.append(
            pltpu.make_async_copy(rhs_hbm.at[0, :, row, :], rhs_ref.at[row], load_sem.at[4 + row])
        )
    for one in loads:
        one.start()

    line = lax.broadcasted_iota(jnp.int32, (6 * TRACE, BLOCK), 0)
    spot = lax.broadcasted_iota(jnp.int32, (6 * TRACE, BLOCK), 1)
    block = line // TRACE
    inner = line - block * TRACE
    var = inner // (NP * NP)
    first = (inner // NP) % NP
    second = inner % NP
    feature = var * (NP * NP * NP)
    last = NP - 1
    along = jnp.where(block == 0, last, 0) * NP * NP + first * NP + second
    cross_x = first * NP * NP + jnp.where(block == 2, last, 0) * NP + second
    cross_y = first * NP * NP + second * NP + jnp.where(block == 4, last, 0)
    is_x = jnp.logical_or(block == 1, block == 2)
    is_y = jnp.logical_or(block == 3, block == 4)
    feature = feature + jnp.where(is_x, cross_x, jnp.where(is_y, cross_y, along))
    picks = jnp.where(spot == feature, 1.0, 0.0).astype(BF16)

    loads[0].wait()
    for kind in range(KD):
        full_ref[:, kind * WIDE : (kind + 1) * WIDE] = table_ref[kind, :, :WIDE]
    for pair in range(KD // 2):
        full_ref[:, KD * WIDE + pair * LANES : KD * WIDE + (pair + 1) * LANES] = jnp.concatenate(
            [table_ref[2 * pair, :, WIDE:], table_ref[2 * pair + 1, :, WIDE:]], axis=1
        )
    for part in range(DEPTH // WIDE):
        lanes = slice(part * WIDE, (part + 1) * WIDE)
        trace_ref[:, lanes] = jnp.dot(
            picks, full_ref[:, lanes], preferred_element_type=F32
        ).astype(BF16)

    loads[1].wait()
    loads[2].wait()
    for row in range(rows):
        group, lanes = row // GROUP, slice(row % GROUP * LANES, (row % GROUP + 1) * LANES)
        kinds = jnp.broadcast_to(kind_ref[row : row + 1, :], (PACK, LANES))
        for kind in range(KD):
            kmask_ref[group, kind, :, lanes] = jnp.where(kinds == kind, 1.0, 0.0).astype(BF16)
        for face in range(6):
            one = jnp.broadcast_to(face_ref[face, row : row + 1, :], (PACK, LANES))
            fmask_ref[group, face, :, lanes] = one.astype(F32).astype(BF16)

    def lay_out_coupling():
        loads[3].wait()
        for face in range(2):
            for kind in range(KC):
                tall_ref[kind * TRACE : (kind + 1) * TRACE, :BLOCK] = coupling_ref[
                    (kind * 6 + face) * TRACE : (kind * 6 + face + 1) * TRACE, :
                ]
            chain_ref[face] = jnp.transpose(tall_ref[: 2 * LANES, :])[:BLOCK, : KC * TRACE]
        for kind in range(KC):
            tall_ref[kind * LATERAL : (kind + 1) * LATERAL, :BLOCK] = coupling_ref[
                (kind * 6 + 2) * TRACE : (kind * 6 + 6) * TRACE, :
            ]
        lat_ref[...] = jnp.transpose(tall_ref[...])[:BLOCK]

    for row in range(rows):
        loads[4 + row].wait()
    pl.semaphore_wait(barrier, total)

    lane = lax.broadcasted_iota(jnp.int32, (TRACE, LANES), 1)
    edges = (jnp.where(lane == 0, 1.0, 0.0), jnp.where(lane == LANES - 1, 1.0, 0.0))
    flip = lax.rem(places["cx"][0], 2)

    def place_of(turn):
        return turn + flip * (groups - 1 - 2 * turn)

    def front_copy(half, group, step):
        return pltpu.make_async_remote_copy(
            src_ref=front_out.at[half, group],
            dst_ref=front_in.at[half, group],
            send_sem=front_send.at[half, group],
            recv_sem=front_recv.at[half, group],
            device_id=partner("sweep", step),
            device_id_type=MESH,
        )

    def x_copy(half, side):
        source, target = (x_low.at[half, 1], x_low.at[half, rows + 1])
        if side == 1:
            source, target = (x_high.at[half, rows], x_high.at[half, 0])
        return pltpu.make_async_remote_copy(
            src_ref=source,
            dst_ref=target,
            send_sem=x_send.at[half, side],
            recv_sem=x_recv.at[half, 1 - side],
            device_id=partner("cx", 2 * side - 1),
            device_id_type=MESH,
        )

    def y_copy(half, side, group):
        return pltpu.make_async_remote_copy(
            src_ref=y_out.at[half, side, group],
            dst_ref=y_in.at[half, 1 - side, group],
            send_sem=y_send.at[half, side, group],
            recv_sem=y_recv.at[half, 1 - side, group],
            device_id=partner("cy", 2 * side - 1),
            device_id_type=MESH,
        )

    def x_here(side, group):
        return jnp.logical_and(has("cx", 2 * side - 1), group == (groups - 1) * side)

    def put_masked(stack, place, lanes, value, mask, apart):
        tiles = value.reshape(-1, PACK, value.shape[-1])
        one = tiles * mask[None]
        stack[place : place + TRACE, lanes] = (tiles - one).reshape(value.shape)
        stack[place + apart : place + apart + TRACE, lanes] = one.reshape(value.shape)

    def turned(value, shift):
        return pltpu.roll(value, shift % LANES, 1) if shift % LANES else value

    def lateral(half, group):
        for side in range(2):

            @pl.when(x_here(side, group))
            def _():
                x_copy(half, 1 - side).wait_recv()

            @pl.when(has("cy", 2 * side - 1))
            def _():
                y_copy(half, 1 - side, group).wait_recv()

        for local in range(GROUP):
            row = group * GROUP + local
            lanes = slice(local * LANES, (local + 1) * LANES)
            values = [x_high[half, row], x_low[half, row + 2]]
            for side in range(2):
                seen = turned(y_in[half, side, group].astype(F32), local * (2 * side - 1))
                own = y_own[half, side, row].astype(F32)
                values.append((own + seen * edges[side]).astype(BF16))
            for face in range(4):
                mask = fmask_ref[group, 2 + face, :, lanes]
                put_masked(lat_stack, face * TRACE, lanes, values[face], mask, LATERAL)
        return jnp.dot(lat_ref[...], lat_stack[...], preferred_element_type=F32)

    def chained(half, group, step, face):
        front_copy(half, group, step).wait_recv()
        put_masked(
            chain_stack, 0, slice(None), front_in[half, group], fmask_ref[group, face], TRACE
        )
        return jnp.dot(chain_ref[face], chain_stack[...], preferred_element_type=F32)

    def rhs_of(group):
        return jnp.concatenate([rhs_ref[group * GROUP + local] for local in range(GROUP)], axis=1)

    def spread(residual, group):
        tiles = residual.astype(BF16).reshape(BLOCK // PACK, PACK, COLS)
        for kind in range(KD):
            masked = (tiles * kmask_ref[group, kind][None]).reshape(BLOCK, COLS)
            rest = KD * WIDE + kind * REST
            inv_stack[kind * WIDE : (kind + 1) * WIDE, :] = masked[:WIDE]
            inv_stack[rest : rest + REST, :] = masked[WIDE:]

    def finish(half, group, downstream):
        forward = half % 2 == 0
        step = 1 if forward else -1
        if half == HALVES - 1:
            updated = jnp.dot(full_ref[...], inv_stack[...], preferred_element_type=F32)
            for local in range(GROUP):
                row = group * GROUP + local
                out_ref[pl.ds(row, BLOCK, stride=rows), :] = updated[
                    :, local * LANES : (local + 1) * LANES
                ]
            front = jnp.concatenate(
                [
                    updated[var * NP * NP * NP : var * NP * NP * NP + NP * NP, :]
                    for var in range(NVAR)
                ],
                axis=0,
            )
            front_out[half, group] = front.astype(BF16)

            @pl.when(downstream)
            def _():
                front_copy(half, group, step).start()

            return
        low = 0 if forward else TRACE
        updated = jnp.dot(
            trace_ref[low : low + 5 * TRACE, :], inv_stack[...], preferred_element_type=F32
        )
        front = 0 if forward else 4 * TRACE
        cross = TRACE if forward else 0
        front_out[half, group] = updated[front : front + TRACE, :].astype(BF16)

        @pl.when(downstream)
        def _():
            front_copy(half, group, step).start()

        for side in range(2):
            start = cross + (2 + side) * TRACE
            packed = jnp.zeros((TRACE, LANES), F32)
            away = 1 - 2 * (1 - side)
            edge = 1 - side
            for local in range(GROUP):
                row = group * GROUP + local
                value = updated[start : start + TRACE, local * LANES : (local + 1) * LANES]
                moved = turned(value, away)
                y_own[half, edge, row] = (moved * (1.0 - edges[edge])).astype(BF16)
                spot = local if side == 1 else LANES - 1 - local
                packed = jnp.where(lane == spot, turned(value, away * (1 + local)), packed)
            y_out[half, side, group] = packed.astype(BF16)

            @pl.when(has("cy", 2 * side - 1))
            def _():
                y_copy(half, side, group).start()

        for local in range(GROUP):
            row = group * GROUP + local
            lanes = slice(local * LANES, (local + 1) * LANES)
            x_low[half, row + 1] = updated[cross : cross + TRACE, lanes].astype(BF16)
            x_high[half, row + 1] = updated[cross + TRACE : cross + 2 * TRACE, lanes].astype(BF16)
        for side in range(2):

            @pl.when(x_here(side, group))
            def _():
                x_copy(half, side).start()

    for half in range(HALVES):
        step = 1 if half % 2 == 0 else -1
        face = 0 if half % 2 == 0 else 1
        upstream = has("sweep", -step)
        downstream = has("sweep", step)

        @pl.when(upstream)
        def _():
            if half == 0:
                lay_out_coupling()
            else:

                @pl.loop(0, groups)
                def _(turn):
                    group = place_of(turn)
                    base_ref[group] = rhs_of(group) - lateral(half - 1, group) - prod_ref[group]

            @pl.loop(0, groups)
            def _(turn):
                group = place_of(turn)
                part = chained(half, group, step, face)
                if half < HALVES - 1:
                    prod_ref[group] = part
                start = rhs_of(group) if half == 0 else base_ref[group]
                spread(start - part, group)
                finish(half, group, downstream)

        @pl.when(jnp.logical_not(upstream))
        def _():
            @pl.loop(0, groups)
            def _(turn):
                group = place_of(turn)
                start = rhs_of(group)
                if half > 0:
                    start = start - lateral(half - 1, group) - prod_ref[group]
                spread(start, group)
                finish(half, group, downstream)
                prod_ref[group] = jnp.zeros((BLOCK, COLS), F32)

            if half == 0:
                lay_out_coupling()

    for half in range(HALVES):
        step = 1 if half % 2 == 0 else -1

        @pl.when(has("sweep", step))
        def _():
            @pl.loop(0, groups)
            def _(group):
                front_copy(half, group, step).wait_send()

        if half < HALVES - 1:
            for side in range(2):

                @pl.when(has("cy", 2 * side - 1))
                def _():
                    @pl.loop(0, groups)
                    def _(group):
                        y_copy(half, side, group).wait_send()

                @pl.when(has("cx", 2 * side - 1))
                def _():
                    x_copy(half, side).wait_send()


def shards(right_side, inverse_table, coupling_table, block_kind, face_kind):
    _, _, rows, width_y = right_side.shape
    groups = rows // GROUP
    result = pl.pallas_call(
        functools.partial(kernel, rows),
        out_shape=jax.ShapeDtypeStruct((BLOCK * rows, LANES), F32),
        in_specs=[pl.BlockSpec(memory_space=pl.ANY)] * 5,
        out_specs=pl.BlockSpec(memory_space=pltpu.VMEM),
        scratch_shapes=[
            pltpu.VMEM((rows, BLOCK, LANES), F32),
            pltpu.VMEM((KD, BLOCK, BLOCK), BF16),
            pltpu.VMEM((KC * 6 * TRACE, BLOCK), BF16),
            pltpu.VMEM((rows, LANES), jnp.int32),
            pltpu.VMEM((6, rows, LANES), jnp.int32),
            pltpu.VMEM((BLOCK, DEPTH), BF16),
            pltpu.VMEM((6 * TRACE, DEPTH), BF16),
            pltpu.VMEM((KC * LATERAL, 3 * LANES), BF16),
            pltpu.VMEM((BLOCK, KC * LATERAL), BF16),
            pltpu.VMEM((2, BLOCK, KC * TRACE), BF16),
            pltpu.VMEM((groups, KD, PACK, COLS), BF16),
            pltpu.VMEM((groups, 6, PACK, COLS), BF16),
            pltpu.VMEM((groups, BLOCK, COLS), F32),
            pltpu.VMEM((groups, BLOCK, COLS), F32),
            pltpu.VMEM((KC * LATERAL, COLS), BF16),
            pltpu.VMEM((KC * TRACE, COLS), BF16),
            pltpu.VMEM((DEPTH, COLS), BF16),
            pltpu.VMEM((HALVES, groups, TRACE, COLS), BF16),
            pltpu.VMEM((HALVES, groups, TRACE, COLS), BF16),
            pltpu.VMEM((HALVES - 1, rows + 2, TRACE, LANES), BF16),
            pltpu.VMEM((HALVES - 1, rows + 2, TRACE, LANES), BF16),
            pltpu.VMEM((HALVES - 1, 2, rows, TRACE, LANES), BF16),
            pltpu.VMEM((HALVES - 1, 2, groups, TRACE, LANES), BF16),
            pltpu.VMEM((HALVES - 1, 2, groups, TRACE, LANES), BF16),
            pltpu.SemaphoreType.DMA((4 + rows,)),
            pltpu.SemaphoreType.DMA((HALVES, groups)),
            pltpu.SemaphoreType.DMA((HALVES, groups)),
            pltpu.SemaphoreType.DMA((HALVES - 1, 2)),
            pltpu.SemaphoreType.DMA((HALVES - 1, 2)),
            pltpu.SemaphoreType.DMA((HALVES - 1, 2, groups)),
            pltpu.SemaphoreType.DMA((HALVES - 1, 2, groups)),
        ],
        compiler_params=pltpu.CompilerParams(
            collective_id=0, has_side_effects=True, vmem_limit_bytes=48 << 20
        ),
    )(
        *[
            pltpu.with_memory_space_constraint(one, pltpu.HBM)
            for one in (
                right_side,
                inverse_table,
                coupling_table.reshape(KC * 6 * TRACE, BLOCK),
                block_kind.reshape(rows, width_y),
                face_kind.reshape(6, rows, width_y),
            )
        ]
    )
    return result.reshape(right_side.shape)


def solution(mesh):
    in_specs = (
        P("sweep", None, "cx", "cy"),
        P(),
        P(),
        P("sweep", "cx", "cy"),
        P("sweep", None, "cx", "cy"),
    )
    out_specs = P("sweep", None, "cx", "cy")
    return jax.shard_map(shards, mesh=mesh, in_specs=in_specs, out_specs=out_specs, check_vma=False)
```

```python
import functools
import jax
import jax.numpy as jnp
from jax import lax
from jax.experimental import pallas as pl
from jax.experimental.pallas import tpu as pltpu
from jax.sharding import PartitionSpec as P

NVAR = 5
NP = 4
BLOCK = 320
TRACE = 80
KD = 4
KC = 2
SWEEPS = 2
HALVES = 2 * SWEEPS
LANES = 128
WIDE = 256
REST = BLOCK - WIDE
GROUP = 2
COLS = GROUP * LANES
DEPTH = KD * BLOCK
LATERAL = 4 * TRACE
PACK = 16
MESH = pl.DeviceIdType.MESH
F32 = jnp.float32
BF16 = jnp.bfloat16


def kernel(
    rows,
    rhs_hbm,
    table_hbm,
    coupling_hbm,
    kind_hbm,
    face_hbm,
    out_ref,
    rhs_ref,
    table_ref,
    coupling_ref,
    kind_ref,
    face_ref,
    full_ref,
    trace_ref,
    tall_ref,
    lat_ref,
    chain_ref,
    kmask_ref,
    fmask_ref,
    prod_ref,
    lat_stack,
    chain_stack,
    inv_stack,
    front_stack,
    ubase_ref,
    g_lat,
    g_front,
    g_full,
    front_in,
    front_out,
    x_low,
    x_high,
    y_own,
    y_in,
    y_out,
    load_sem,
    front_send,
    front_recv,
    x_send,
    x_recv,
    y_send,
    y_recv,
):
    groups = rows // GROUP
    places = {}
    for name in ("sweep", "cx", "cy"):
        places[name] = (lax.axis_index(name), lax.axis_size(name))

    def has(name, step):
        spot, count = places[name]
        return spot < count - 1 if step > 0 else spot > 0

    def partner(name, step):
        return {name: places[name][0] + step}

    for half in range(HALVES - 1):
        x_high[half, 0] = jnp.zeros((TRACE, LANES), BF16)
        x_low[half, rows + 1] = jnp.zeros((TRACE, LANES), BF16)
    for side in range(2):

        @pl.when(jnp.logical_not(has("cy", 2 * side - 1)))
        def _():
            for half in range(HALVES - 1):
                y_in[half, side] = jnp.zeros((groups, TRACE, LANES), BF16)

    barrier = pltpu.get_barrier_semaphore()
    total = 0
    for name in ("sweep", "cx", "cy"):
        for step in (-1, 1):
            exists = has(name, step)
            total = total + jnp.where(exists, 1, 0)

            @pl.when(exists)
            def _():
                pl.semaphore_signal(
                    barrier, inc=1, device_id=partner(name, step), device_id_type=MESH
                )

    loads = [
        pltpu.make_async_copy(table_hbm, table_ref, load_sem.at[0]),
        pltpu.make_async_copy(kind_hbm, kind_ref, load_sem.at[1]),
        pltpu.make_async_copy(face_hbm, face_ref, load_sem.at[2]),
        pltpu.make_async_copy(coupling_hbm, coupling_ref, load_sem.at[3]),
    ]
    for row in range(rows):
        loads.append(
            pltpu.make_async_copy(rhs_hbm.at[0, :, row, :], rhs_ref.at[row], load_sem.at[4 + row])
        )
    for one in loads:
        one.start()

    def picks(start, count):
        line = lax.broadcasted_iota(jnp.int32, (count, BLOCK), 0) + start
        spot = lax.broadcasted_iota(jnp.int32, (count, BLOCK), 1)
        block = line // TRACE
        inner = line - block * TRACE
        var = inner // (NP * NP)
        first = (inner // NP) % NP
        second = inner % NP
        last = NP - 1
        along = jnp.where(block == 0, last, 0) * NP * NP + first * NP + second
        cross_x = first * NP * NP + jnp.where(block == 2, last, 0) * NP + second
        cross_y = first * NP * NP + second * NP + jnp.where(block == 4, last, 0)
        is_x = jnp.logical_or(block == 1, block == 2)
        is_y = jnp.logical_or(block == 3, block == 4)
        feature = jnp.where(is_x, cross_x, jnp.where(is_y, cross_y, along))
        feature = feature + var * (NP * NP * NP)
        return jnp.where(spot == feature, 1.0, 0.0).astype(BF16)

    def pick_rows(chosen, start, count):
        for part in range(DEPTH // WIDE):
            lanes = slice(part * WIDE, (part + 1) * WIDE)
            trace_ref[start : start + count, lanes] = jnp.dot(
                chosen, full_ref[:, lanes], preferred_element_type=F32
            ).astype(BF16)

    some = picks(0, TRACE)
    loads[0].wait()
    for kind in range(KD):
        full_ref[:, kind * WIDE : (kind + 1) * WIDE] = table_ref[kind, :, :WIDE]
    for pair in range(KD // 2):
        full_ref[:, KD * WIDE + pair * LANES : KD * WIDE + (pair + 1) * LANES] = jnp.concatenate(
            [table_ref[2 * pair, :, WIDE:], table_ref[2 * pair + 1, :, WIDE:]], axis=1
        )
    pick_rows(some, 0, TRACE)

    loads[1].wait()
    loads[2].wait()
    for row in range(rows):
        group, lanes = row // GROUP, slice(row % GROUP * LANES, (row % GROUP + 1) * LANES)
        kinds = jnp.broadcast_to(kind_ref[row : row + 1, :], (PACK, LANES))
        for kind in range(KD):
            kmask_ref[group, kind, :, lanes] = jnp.where(kinds == kind, 1.0, 0.0).astype(BF16)
        for face in range(6):
            one = jnp.broadcast_to(face_ref[face, row : row + 1, :], (PACK, LANES))
            fmask_ref[group, face, :, lanes] = one.astype(F32).astype(BF16)

    def lay_out_coupling():
        loads[3].wait()
        for face in range(2):
            for kind in range(KC):
                tall_ref[kind * TRACE : (kind + 1) * TRACE, :BLOCK] = coupling_ref[
                    (kind * 6 + face) * TRACE : (kind * 6 + face + 1) * TRACE, :
                ]
            chain_ref[face] = jnp.transpose(tall_ref[: 2 * LANES, :])[:BLOCK, : KC * TRACE]
        for kind in range(KC):
            tall_ref[kind * LATERAL : (kind + 1) * LATERAL, :BLOCK] = coupling_ref[
                (kind * 6 + 2) * TRACE : (kind * 6 + 6) * TRACE, :
            ]
        lat_ref[...] = jnp.transpose(tall_ref[...])[:BLOCK]

    def corrected(rows_ref, start, count, face, target):
        for kind in range(KD):
            low, rest = kind * WIDE, KD * WIDE + kind * REST
            value = jnp.dot(
                rows_ref[start : start + count, low : low + WIDE],
                chain_ref[face, :WIDE, :],
                preferred_element_type=F32,
            ) + jnp.dot(
                rows_ref[start : start + count, rest : rest + REST],
                chain_ref[face, WIDE:, :],
                preferred_element_type=F32,
            )
            target[:, kind * KC * TRACE : (kind + 1) * KC * TRACE] = value.astype(BF16)

    for row in range(rows):
        loads[4 + row].wait()
    pl.semaphore_wait(barrier, total)

    lane = lax.broadcasted_iota(jnp.int32, (TRACE, LANES), 1)
    edges = (jnp.where(lane == 0, 1.0, 0.0), jnp.where(lane == LANES - 1, 1.0, 0.0))
    flip = lax.rem(places["cx"][0], 2)

    def place_of(turn):
        return turn + flip * (groups - 1 - 2 * turn)

    def front_copy(half, group, step):
        return pltpu.make_async_remote_copy(
            src_ref=front_out.at[half, group],
            dst_ref=front_in.at[half, group],
            send_sem=front_send.at[half, group],
            recv_sem=front_recv.at[half, group],
            device_id=partner("sweep", step),
            device_id_type=MESH,
        )

    def x_copy(half, side):
        source, target = (x_low.at[half, 1], x_low.at[half, rows + 1])
        if side == 1:
            source, target = (x_high.at[half, rows], x_high.at[half, 0])
        return pltpu.make_async_remote_copy(
            src_ref=source,
            dst_ref=target,
            send_sem=x_send.at[half, side],
            recv_sem=x_recv.at[half, 1 - side],
            device_id=partner("cx", 2 * side - 1),
            device_id_type=MESH,
        )

    def y_copy(half, side, group):
        return pltpu.make_async_remote_copy(
            src_ref=y_out.at[half, side, group],
            dst_ref=y_in.at[half, 1 - side, group],
            send_sem=y_send.at[half, side, group],
            recv_sem=y_recv.at[half, 1 - side, group],
            device_id=partner("cy", 2 * side - 1),
            device_id_type=MESH,
        )

    def x_here(side, group):
        return jnp.logical_and(has("cx", 2 * side - 1), group == (groups - 1) * side)

    def put_masked(stack, place, lanes, value, mask, apart):
        tiles = value.reshape(-1, PACK, value.shape[-1])
        one = tiles * mask[None]
        stack[place : place + TRACE, lanes] = (tiles - one).reshape(value.shape)
        stack[place + apart : place + apart + TRACE, lanes] = one.reshape(value.shape)

    def turned(value, shift):
        return pltpu.roll(value, shift % LANES, 1) if shift % LANES else value

    def lateral(half, group):
        for side in range(2):

            @pl.when(x_here(side, group))
            def _():
                x_copy(half, 1 - side).wait_recv()

            @pl.when(has("cy", 2 * side - 1))
            def _():
                y_copy(half, 1 - side, group).wait_recv()

        for local in range(GROUP):
            row = group * GROUP + local
            lanes = slice(local * LANES, (local + 1) * LANES)
            values = [x_high[half, row], x_low[half, row + 2]]
            for side in range(2):
                seen = turned(y_in[half, side, group].astype(F32), local * (2 * side - 1))
                own = y_own[half, side, row].astype(F32)
                values.append((own + seen * edges[side]).astype(BF16))
            for face in range(4):
                mask = fmask_ref[group, 2 + face, :, lanes]
                put_masked(lat_stack, face * TRACE, lanes, values[face], mask, LATERAL)
        return jnp.dot(lat_ref[...], lat_stack[...], preferred_element_type=F32)

    def product_of(half, group, face):
        put_masked(
            chain_stack, 0, slice(None), front_in[half, group], fmask_ref[group, face], TRACE
        )
        return jnp.dot(chain_ref[face], chain_stack[...], preferred_element_type=F32)

    def rhs_of(group):
        return jnp.concatenate([rhs_ref[group * GROUP + local] for local in range(GROUP)], axis=1)

    def spread(residual, group):
        tiles = residual.astype(BF16).reshape(BLOCK // PACK, PACK, COLS)
        for kind in range(KD):
            masked = (tiles * kmask_ref[group, kind][None]).reshape(BLOCK, COLS)
            rest = KD * WIDE + kind * REST
            inv_stack[group, kind * WIDE : (kind + 1) * WIDE, :] = masked[:WIDE]
            inv_stack[group, rest : rest + REST, :] = masked[WIDE:]

    def inverse_rows(rows_ref, start, count, group):
        return jnp.dot(
            rows_ref[start : start + count, :], inv_stack[group], preferred_element_type=F32
        )

    def spread_front(half, group, face):
        seen = front_in[half, group].reshape(TRACE // PACK, PACK, COLS)
        high = seen * fmask_ref[group, face][None]
        parts = (seen - high, high)
        for kind in range(KD):
            for which in range(KC):
                place = (kind * KC + which) * TRACE
                one = parts[which] * kmask_ref[group, kind][None]
                front_stack[place : place + TRACE, :] = one.reshape(TRACE, COLS)

    def correction(table):
        return jnp.dot(table, front_stack[...], preferred_element_type=F32)

    def put_out(group, value):
        for local in range(GROUP):
            row = group * GROUP + local
            out_ref[pl.ds(row, BLOCK, stride=rows), :] = value[
                :, local * LANES : (local + 1) * LANES
            ]

    def send_front(half, group, step, value):
        front_out[half, group] = value.astype(BF16)
        front_copy(half, group, step).start()

    def emit(half, group, value):
        for side in range(2):
            start = (2 + side) * TRACE
            packed = jnp.zeros((TRACE, LANES), F32)
            away = 1 - 2 * (1 - side)
            edge = 1 - side
            for local in range(GROUP):
                row = group * GROUP + local
                one = value[start : start + TRACE, local * LANES : (local + 1) * LANES]
                moved = turned(one, away)
                y_own[half, edge, row] = (moved * (1.0 - edges[edge])).astype(BF16)
                spot = local if side == 1 else LANES - 1 - local
                packed = jnp.where(lane == spot, turned(one, away * (1 + local)), packed)
            y_out[half, side, group] = packed.astype(BF16)

            @pl.when(has("cy", 2 * side - 1))
            def _():
                y_copy(half, side, group).start()

        for local in range(GROUP):
            row = group * GROUP + local
            lanes = slice(local * LANES, (local + 1) * LANES)
            x_low[half, row + 1] = value[:TRACE, lanes].astype(BF16)
            x_high[half, row + 1] = value[TRACE : 2 * TRACE, lanes].astype(BF16)
        for side in range(2):

            @pl.when(x_here(side, group))
            def _():
                x_copy(half, side).start()

    def each_group(body):
        @pl.loop(0, groups)
        def _(turn):
            body(place_of(turn))

    def set_up_rest():
        lay_out_coupling()
        pick_rows(picks(TRACE, 5 * TRACE), TRACE, 5 * TRACE)

        @pl.when(has("sweep", -1))
        def _():
            corrected(trace_ref, TRACE, LATERAL, 0, g_lat.at[0])

            @pl.when(has("sweep", 1))
            def _():
                corrected(trace_ref, 0, TRACE, 0, g_front.at[0])

    def set_up_back():
        @pl.when(has("sweep", 1))
        def _():
            corrected(trace_ref, TRACE, LATERAL, 1, g_lat.at[1])
            corrected(full_ref, 0, BLOCK, 1, g_full)

            @pl.when(has("sweep", -1))
            def _():
                corrected(trace_ref, 5 * TRACE, TRACE, 1, g_front.at[1])

    for half in range(HALVES):
        step = 1 if half % 2 == 0 else -1
        face = 0 if half % 2 == 0 else 1
        front_rows = 0 if half % 2 == 0 else 5 * TRACE
        final = half == HALVES - 1
        upstream = has("sweep", -step)
        downstream = has("sweep", step)

        def start_of(group):
            start = rhs_of(group)
            if half > 0:
                start = start - lateral(half - 1, group) - prod_ref[group]
            return start

        @pl.when(jnp.logical_not(upstream))
        def _():
            def first_part(group):
                spread(start_of(group), group)

                @pl.when(downstream)
                def _():
                    send_front(half, group, step, inverse_rows(trace_ref, front_rows, TRACE, group))

            each_group(first_part)

        if half == 0:
            set_up_rest()

        @pl.when(jnp.logical_not(upstream))
        def _():
            def second_part(group):
                if final:
                    put_out(group, inverse_rows(full_ref, 0, BLOCK, group))
                else:
                    emit(half, group, inverse_rows(trace_ref, TRACE, LATERAL, group))
                    prod_ref[group] = jnp.zeros((BLOCK, COLS), F32)

            each_group(second_part)

        if half == 0:
            set_up_back()

        @pl.when(upstream)
        def _():
            def before(group):
                spread(start_of(group), group)
                if final:
                    ubase_ref[group, :BLOCK] = inverse_rows(full_ref, 0, BLOCK, group)
                else:
                    ubase_ref[group, :LATERAL] = inverse_rows(trace_ref, TRACE, LATERAL, group)

                @pl.when(downstream)
                def _():
                    ubase_ref[group, LATERAL:] = inverse_rows(trace_ref, front_rows, TRACE, group)

            def arrived(group):
                front_copy(half, group, step).wait_recv()
                spread_front(half, group, face)

                @pl.when(downstream)
                def _():
                    send_front(
                        half, group, step, ubase_ref[group, LATERAL:] - correction(g_front[face])
                    )

                if final:
                    put_out(group, ubase_ref[group, :BLOCK] - correction(g_full[...]))
                else:
                    emit(half, group, ubase_ref[group, :LATERAL] - correction(g_lat[face]))

            def after(group):
                prod_ref[group] = product_of(half, group, face)

            each_group(before)
            each_group(arrived)
            if not final:
                each_group(after)

    for half in range(HALVES):
        step = 1 if half % 2 == 0 else -1

        @pl.when(has("sweep", step))
        def _():
            @pl.loop(0, groups)
            def _(group):
                front_copy(half, group, step).wait_send()

        if half < HALVES - 1:
            for side in range(2):

                @pl.when(has("cy", 2 * side - 1))
                def _():
                    @pl.loop(0, groups)
                    def _(group):
                        y_copy(half, side, group).wait_send()

                @pl.when(has("cx", 2 * side - 1))
                def _():
                    x_copy(half, side).wait_send()


def shards(right_side, inverse_table, coupling_table, block_kind, face_kind):
    _, _, rows, width_y = right_side.shape
    groups = rows // GROUP
    result = pl.pallas_call(
        functools.partial(kernel, rows),
        out_shape=jax.ShapeDtypeStruct((BLOCK * rows, LANES), F32),
        in_specs=[pl.BlockSpec(memory_space=pl.ANY)] * 5,
        out_specs=pl.BlockSpec(memory_space=pltpu.VMEM),
        scratch_shapes=[
            pltpu.VMEM((rows, BLOCK, LANES), F32),
            pltpu.VMEM((KD, BLOCK, BLOCK), BF16),
            pltpu.VMEM((KC * 6 * TRACE, BLOCK), BF16),
            pltpu.VMEM((rows, LANES), jnp.int32),
            pltpu.VMEM((6, rows, LANES), jnp.int32),
            pltpu.VMEM((BLOCK, DEPTH), BF16),
            pltpu.VMEM((6 * TRACE, DEPTH), BF16),
            pltpu.VMEM((KC * LATERAL, 3 * LANES), BF16),
            pltpu.VMEM((BLOCK, KC * LATERAL), BF16),
            pltpu.VMEM((2, BLOCK, KC * TRACE), BF16),
            pltpu.VMEM((groups, KD, PACK, COLS), BF16),
            pltpu.VMEM((groups, 6, PACK, COLS), BF16),
            pltpu.VMEM((groups, BLOCK, COLS), F32),
            pltpu.VMEM((KC * LATERAL, COLS), BF16),
            pltpu.VMEM((KC * TRACE, COLS), BF16),
            pltpu.VMEM((groups, DEPTH, COLS), BF16),
            pltpu.VMEM((KD * KC * TRACE, COLS), BF16),
            pltpu.VMEM((groups, LATERAL + TRACE, COLS), F32),
            pltpu.VMEM((2, LATERAL, KD * KC * TRACE), BF16),
            pltpu.VMEM((2, TRACE, KD * KC * TRACE), BF16),
            pltpu.VMEM((BLOCK, KD * KC * TRACE), BF16),
            pltpu.VMEM((HALVES, groups, TRACE, COLS), BF16),
            pltpu.VMEM((HALVES, groups, TRACE, COLS), BF16),
            pltpu.VMEM((HALVES - 1, rows + 2, TRACE, LANES), BF16),
            pltpu.VMEM((HALVES - 1, rows + 2, TRACE, LANES), BF16),
            pltpu.VMEM((HALVES - 1, 2, rows, TRACE, LANES), BF16),
            pltpu.VMEM((HALVES - 1, 2, groups, TRACE, LANES), BF16),
            pltpu.VMEM((HALVES - 1, 2, groups, TRACE, LANES), BF16),
            pltpu.SemaphoreType.DMA((4 + rows,)),
            pltpu.SemaphoreType.DMA((HALVES, groups)),
            pltpu.SemaphoreType.DMA((HALVES, groups)),
            pltpu.SemaphoreType.DMA((HALVES - 1, 2)),
            pltpu.SemaphoreType.DMA((HALVES - 1, 2)),
            pltpu.SemaphoreType.DMA((HALVES - 1, 2, groups)),
            pltpu.SemaphoreType.DMA((HALVES - 1, 2, groups)),
        ],
        compiler_params=pltpu.CompilerParams(
            collective_id=0, has_side_effects=True, vmem_limit_bytes=48 << 20
        ),
    )(
        *[
            pltpu.with_memory_space_constraint(one, pltpu.HBM)
            for one in (
                right_side,
                inverse_table,
                coupling_table.reshape(KC * 6 * TRACE, BLOCK),
                block_kind.reshape(rows, width_y),
                face_kind.reshape(6, rows, width_y),
            )
        ]
    )
    return result.reshape(right_side.shape)


def solution(mesh):
    in_specs = (
        P("sweep", None, "cx", "cy"),
        P(),
        P(),
        P("sweep", "cx", "cy"),
        P("sweep", None, "cx", "cy"),
    )
    out_specs = P("sweep", None, "cx", "cy")
    return jax.shard_map(shards, mesh=mesh, in_specs=in_specs, out_specs=out_specs, check_vma=False)
```

```python
import functools
import jax
import jax.numpy as jnp
from jax import lax
from jax.experimental import pallas as pl
from jax.experimental.pallas import tpu as pltpu
from jax.sharding import PartitionSpec as P

NVAR = 5
NP = 4
BLOCK = 320
TRACE = 80
KD = 4
KC = 2
SWEEPS = 2
HALVES = 2 * SWEEPS
LANES = 128
WIDE = 256
REST = BLOCK - WIDE
GROUP = 2
COLS = GROUP * LANES
DEPTH = KD * BLOCK
LATERAL = 4 * TRACE
PACK = 16
MESH = pl.DeviceIdType.MESH
F32 = jnp.float32
BF16 = jnp.bfloat16


def kernel(
    rows,
    rhs_hbm,
    table_hbm,
    coupling_hbm,
    kind_hbm,
    face_hbm,
    out_ref,
    rhs_ref,
    table_ref,
    coupling_ref,
    kind_ref,
    face_ref,
    full_ref,
    trace_ref,
    tall_ref,
    lat_ref,
    chain_ref,
    kmask_ref,
    fmask_ref,
    prod_ref,
    lat_stack,
    chain_stack,
    inv_stack,
    front_stack,
    ubase_ref,
    g_lat,
    g_front,
    g_full,
    front_in,
    front_out,
    x_low,
    x_high,
    y_own,
    y_in,
    y_out,
    load_sem,
    front_send,
    front_recv,
    x_send,
    x_recv,
    y_send,
    y_recv,
):
    groups = rows // GROUP
    places = {}
    for name in ("sweep", "cx", "cy"):
        places[name] = (lax.axis_index(name), lax.axis_size(name))

    def has(name, step):
        spot, count = places[name]
        return spot < count - 1 if step > 0 else spot > 0

    def partner(name, step):
        return {name: places[name][0] + step}

    for half in range(HALVES - 1):
        x_high[half, 0] = jnp.zeros((TRACE, LANES), BF16)
        x_low[half, rows + 1] = jnp.zeros((TRACE, LANES), BF16)
    for side in range(2):

        @pl.when(jnp.logical_not(has("cy", 2 * side - 1)))
        def _():
            for half in range(HALVES - 1):
                y_in[half, side] = jnp.zeros((groups, TRACE, LANES), BF16)

    barrier = pltpu.get_barrier_semaphore()
    total = 0
    for name in ("sweep", "cx", "cy"):
        for step in (-1, 1):
            exists = has(name, step)
            total = total + jnp.where(exists, 1, 0)

            @pl.when(exists)
            def _():
                pl.semaphore_signal(
                    barrier, inc=1, device_id=partner(name, step), device_id_type=MESH
                )

    loads = [
        pltpu.make_async_copy(table_hbm, table_ref, load_sem.at[0]),
        pltpu.make_async_copy(kind_hbm, kind_ref, load_sem.at[1]),
        pltpu.make_async_copy(face_hbm, face_ref, load_sem.at[2]),
        pltpu.make_async_copy(coupling_hbm, coupling_ref, load_sem.at[3]),
    ]
    for row in range(rows):
        loads.append(
            pltpu.make_async_copy(rhs_hbm.at[0, :, row, :], rhs_ref.at[row], load_sem.at[4 + row])
        )
    for one in loads:
        one.start()

    def picks(start, count):
        line = lax.broadcasted_iota(jnp.int32, (count, BLOCK), 0) + start
        spot = lax.broadcasted_iota(jnp.int32, (count, BLOCK), 1)
        block = line // TRACE
        inner = line - block * TRACE
        var = inner // (NP * NP)
        first = (inner // NP) % NP
        second = inner % NP
        last = NP - 1
        along = jnp.where(block == 0, last, 0) * NP * NP + first * NP + second
        cross_x = first * NP * NP + jnp.where(block == 2, last, 0) * NP + second
        cross_y = first * NP * NP + second * NP + jnp.where(block == 4, last, 0)
        is_x = jnp.logical_or(block == 1, block == 2)
        is_y = jnp.logical_or(block == 3, block == 4)
        feature = jnp.where(is_x, cross_x, jnp.where(is_y, cross_y, along))
        feature = feature + var * (NP * NP * NP)
        return jnp.where(spot == feature, 1.0, 0.0).astype(BF16)

    def pick_rows(chosen, start, count):
        for part in range(DEPTH // WIDE):
            lanes = slice(part * WIDE, (part + 1) * WIDE)
            trace_ref[start : start + count, lanes] = jnp.dot(
                chosen, full_ref[:, lanes], preferred_element_type=F32
            ).astype(BF16)

    some = picks(0, TRACE)
    loads[0].wait()
    for kind in range(KD):
        full_ref[:, kind * WIDE : (kind + 1) * WIDE] = table_ref[kind, :, :WIDE]
    for pair in range(KD // 2):
        full_ref[:, KD * WIDE + pair * LANES : KD * WIDE + (pair + 1) * LANES] = jnp.concatenate(
            [table_ref[2 * pair, :, WIDE:], table_ref[2 * pair + 1, :, WIDE:]], axis=1
        )
    pick_rows(some, 0, TRACE)

    loads[1].wait()
    loads[2].wait()
    for row in range(rows):
        group, lanes = row // GROUP, slice(row % GROUP * LANES, (row % GROUP + 1) * LANES)
        kinds = jnp.broadcast_to(kind_ref[row : row + 1, :], (PACK, LANES))
        for kind in range(KD):
            kmask_ref[group, kind, :, lanes] = jnp.where(kinds == kind, 1.0, 0.0).astype(BF16)
        for face in range(6):
            one = jnp.broadcast_to(face_ref[face, row : row + 1, :], (PACK, LANES))
            fmask_ref[group, face, :, lanes] = one.astype(F32).astype(BF16)

    def lay_out_coupling():
        loads[3].wait()
        for face in range(2):
            for kind in range(KC):
                tall_ref[kind * TRACE : (kind + 1) * TRACE, :BLOCK] = coupling_ref[
                    (kind * 6 + face) * TRACE : (kind * 6 + face + 1) * TRACE, :
                ]
            chain_ref[face] = jnp.transpose(tall_ref[: 2 * LANES, :])[:BLOCK, : KC * TRACE]
        for kind in range(KC):
            tall_ref[kind * LATERAL : (kind + 1) * LATERAL, :BLOCK] = coupling_ref[
                (kind * 6 + 2) * TRACE : (kind * 6 + 6) * TRACE, :
            ]
        lat_ref[...] = jnp.transpose(tall_ref[...])[:BLOCK]

    def corrected(rows_ref, start, count, face, target):
        for kind in range(KD):
            low, rest = kind * WIDE, KD * WIDE + kind * REST
            value = jnp.dot(
                rows_ref[start : start + count, low : low + WIDE],
                chain_ref[face, :WIDE, :],
                preferred_element_type=F32,
            ) + jnp.dot(
                rows_ref[start : start + count, rest : rest + REST],
                chain_ref[face, WIDE:, :],
                preferred_element_type=F32,
            )
            target[:, kind * KC * TRACE : (kind + 1) * KC * TRACE] = value.astype(BF16)

    for row in range(rows):
        loads[4 + row].wait()
    pl.semaphore_wait(barrier, total)

    lane = lax.broadcasted_iota(jnp.int32, (TRACE, LANES), 1)
    edges = (jnp.where(lane == 0, 1.0, 0.0), jnp.where(lane == LANES - 1, 1.0, 0.0))
    flip = lax.rem(places["cx"][0], 2)

    def place_of(turn):
        group = jnp.where(turn == 0, 0, jnp.where(turn == 1, groups - 1, turn - 1))
        return group + flip * (groups - 1 - 2 * group)

    def front_copy(half, group, step):
        return pltpu.make_async_remote_copy(
            src_ref=front_out.at[half, group],
            dst_ref=front_in.at[half, group],
            send_sem=front_send.at[half, group],
            recv_sem=front_recv.at[half, group],
            device_id=partner("sweep", step),
            device_id_type=MESH,
        )

    def x_copy(half, side):
        source, target = (x_low.at[half, 1], x_low.at[half, rows + 1])
        if side == 1:
            source, target = (x_high.at[half, rows], x_high.at[half, 0])
        return pltpu.make_async_remote_copy(
            src_ref=source,
            dst_ref=target,
            send_sem=x_send.at[half, side],
            recv_sem=x_recv.at[half, 1 - side],
            device_id=partner("cx", 2 * side - 1),
            device_id_type=MESH,
        )

    def y_copy(half, side, group):
        return pltpu.make_async_remote_copy(
            src_ref=y_out.at[half, side, group],
            dst_ref=y_in.at[half, 1 - side, group],
            send_sem=y_send.at[half, side, group],
            recv_sem=y_recv.at[half, 1 - side, group],
            device_id=partner("cy", 2 * side - 1),
            device_id_type=MESH,
        )

    def x_here(side, group):
        return jnp.logical_and(has("cx", 2 * side - 1), group == (groups - 1) * side)

    def put_masked(stack, place, lanes, value, mask, apart):
        tiles = value.reshape(-1, PACK, value.shape[-1])
        one = tiles * mask[None]
        stack[place : place + TRACE, lanes] = (tiles - one).reshape(value.shape)
        stack[place + apart : place + apart + TRACE, lanes] = one.reshape(value.shape)

    def turned(value, shift):
        return pltpu.roll(value, shift % LANES, 1) if shift % LANES else value

    def lateral(half, group):
        for side in range(2):

            @pl.when(x_here(side, group))
            def _():
                x_copy(half, 1 - side).wait_recv()

            @pl.when(has("cy", 2 * side - 1))
            def _():
                y_copy(half, 1 - side, group).wait_recv()

        for local in range(GROUP):
            row = group * GROUP + local
            lanes = slice(local * LANES, (local + 1) * LANES)
            values = [x_high[half, row], x_low[half, row + 2]]
            for side in range(2):
                seen = turned(y_in[half, side, group].astype(F32), local * (2 * side - 1))
                own = y_own[half, side, row].astype(F32)
                values.append((own + seen * edges[side]).astype(BF16))
            for face in range(4):
                mask = fmask_ref[group, 2 + face, :, lanes]
                put_masked(lat_stack, face * TRACE, lanes, values[face], mask, LATERAL)
        return jnp.dot(lat_ref[...], lat_stack[...], preferred_element_type=F32)

    def product_of(half, group, face):
        put_masked(
            chain_stack, 0, slice(None), front_in[half, group], fmask_ref[group, face], TRACE
        )
        return jnp.dot(chain_ref[face], chain_stack[...], preferred_element_type=F32)

    def rhs_of(group):
        return jnp.concatenate([rhs_ref[group * GROUP + local] for local in range(GROUP)], axis=1)

    def spread(residual, group):
        tiles = residual.astype(BF16).reshape(BLOCK // PACK, PACK, COLS)
        for kind in range(KD):
            masked = (tiles * kmask_ref[group, kind][None]).reshape(BLOCK, COLS)
            rest = KD * WIDE + kind * REST
            inv_stack[group, kind * WIDE : (kind + 1) * WIDE, :] = masked[:WIDE]
            inv_stack[group, rest : rest + REST, :] = masked[WIDE:]

    def inverse_rows(rows_ref, start, count, group):
        return jnp.dot(
            rows_ref[start : start + count, :], inv_stack[group], preferred_element_type=F32
        )

    def spread_front(half, group, face):
        seen = front_in[half, group].reshape(TRACE // PACK, PACK, COLS)
        high = seen * fmask_ref[group, face][None]
        parts = (seen - high, high)
        for kind in range(KD):
            for which in range(KC):
                place = (kind * KC + which) * TRACE
                one = parts[which] * kmask_ref[group, kind][None]
                front_stack[place : place + TRACE, :] = one.reshape(TRACE, COLS)

    def correction(table):
        return jnp.dot(table, front_stack[...], preferred_element_type=F32)

    def put_out(group, value):
        for local in range(GROUP):
            row = group * GROUP + local
            out_ref[pl.ds(row, BLOCK, stride=rows), :] = value[
                :, local * LANES : (local + 1) * LANES
            ]

    def send_front(half, group, step, value):
        front_out[half, group] = value.astype(BF16)
        front_copy(half, group, step).start()

    def emit(half, group, value):
        for local in range(GROUP):
            row = group * GROUP + local
            lanes = slice(local * LANES, (local + 1) * LANES)
            x_low[half, row + 1] = value[:TRACE, lanes].astype(BF16)
            x_high[half, row + 1] = value[TRACE : 2 * TRACE, lanes].astype(BF16)
        for side in range(2):

            @pl.when(x_here(side, group))
            def _():
                x_copy(half, side).start()

        for side in range(2):
            start = (2 + side) * TRACE
            packed = jnp.zeros((TRACE, LANES), F32)
            away = 1 - 2 * (1 - side)
            edge = 1 - side
            for local in range(GROUP):
                row = group * GROUP + local
                one = value[start : start + TRACE, local * LANES : (local + 1) * LANES]
                moved = turned(one, away)
                y_own[half, edge, row] = (moved * (1.0 - edges[edge])).astype(BF16)
                spot = local if side == 1 else LANES - 1 - local
                packed = jnp.where(lane == spot, turned(one, away * (1 + local)), packed)
            y_out[half, side, group] = packed.astype(BF16)

            @pl.when(has("cy", 2 * side - 1))
            def _():
                y_copy(half, side, group).start()

    def each_group(body):
        @pl.loop(0, groups)
        def _(turn):
            body(place_of(turn))

    def set_up_rest():
        lay_out_coupling()
        pick_rows(picks(TRACE, 5 * TRACE), TRACE, 5 * TRACE)

        @pl.when(has("sweep", -1))
        def _():
            corrected(trace_ref, TRACE, LATERAL, 0, g_lat.at[0])

            @pl.when(has("sweep", 1))
            def _():
                corrected(trace_ref, 0, TRACE, 0, g_front.at[0])

    def set_up_back():
        @pl.when(has("sweep", 1))
        def _():
            corrected(trace_ref, TRACE, LATERAL, 1, g_lat.at[1])
            corrected(full_ref, 0, BLOCK, 1, g_full)

            @pl.when(has("sweep", -1))
            def _():
                corrected(trace_ref, 5 * TRACE, TRACE, 1, g_front.at[1])

    for half in range(HALVES):
        step = 1 if half % 2 == 0 else -1
        face = 0 if half % 2 == 0 else 1
        front_rows = 0 if half % 2 == 0 else 5 * TRACE
        final = half == HALVES - 1
        upstream = has("sweep", -step)
        downstream = has("sweep", step)

        def start_of(group):
            start = rhs_of(group)
            if half > 0:
                start = start - lateral(half - 1, group) - prod_ref[group]
            return start

        @pl.when(jnp.logical_not(upstream))
        def _():
            def first_part(group):
                spread(start_of(group), group)

                @pl.when(downstream)
                def _():
                    send_front(half, group, step, inverse_rows(trace_ref, front_rows, TRACE, group))

            each_group(first_part)

        if half == 0:
            set_up_rest()

        @pl.when(jnp.logical_not(upstream))
        def _():
            def second_part(group):
                if final:
                    put_out(group, inverse_rows(full_ref, 0, BLOCK, group))
                else:
                    emit(half, group, inverse_rows(trace_ref, TRACE, LATERAL, group))
                    prod_ref[group] = jnp.zeros((BLOCK, COLS), F32)

            each_group(second_part)

        if half == 0:
            set_up_back()

        @pl.when(upstream)
        def _():
            def before(group):
                spread(start_of(group), group)
                if final:
                    ubase_ref[group, :BLOCK] = inverse_rows(full_ref, 0, BLOCK, group)
                else:
                    ubase_ref[group, :LATERAL] = inverse_rows(trace_ref, TRACE, LATERAL, group)

                @pl.when(downstream)
                def _():
                    ubase_ref[group, LATERAL:] = inverse_rows(trace_ref, front_rows, TRACE, group)

            def arrived(group):
                front_copy(half, group, step).wait_recv()
                spread_front(half, group, face)

                @pl.when(downstream)
                def _():
                    send_front(
                        half, group, step, ubase_ref[group, LATERAL:] - correction(g_front[face])
                    )

                if final:
                    put_out(group, ubase_ref[group, :BLOCK] - correction(g_full[...]))
                else:
                    emit(half, group, ubase_ref[group, :LATERAL] - correction(g_lat[face]))

            def after(group):
                prod_ref[group] = product_of(half, group, face)

            each_group(before)
            each_group(arrived)
            if not final:
                each_group(after)

    for half in range(HALVES):
        step = 1 if half % 2 == 0 else -1

        @pl.when(has("sweep", step))
        def _():
            @pl.loop(0, groups)
            def _(group):
                front_copy(half, group, step).wait_send()

        if half < HALVES - 1:
            for side in range(2):

                @pl.when(has("cy", 2 * side - 1))
                def _():
                    @pl.loop(0, groups)
                    def _(group):
                        y_copy(half, side, group).wait_send()

                @pl.when(has("cx", 2 * side - 1))
                def _():
                    x_copy(half, side).wait_send()


def shards(right_side, inverse_table, coupling_table, block_kind, face_kind):
    _, _, rows, width_y = right_side.shape
    groups = rows // GROUP
    result = pl.pallas_call(
        functools.partial(kernel, rows),
        out_shape=jax.ShapeDtypeStruct((BLOCK * rows, LANES), F32),
        in_specs=[pl.BlockSpec(memory_space=pl.ANY)] * 5,
        out_specs=pl.BlockSpec(memory_space=pltpu.VMEM),
        scratch_shapes=[
            pltpu.VMEM((rows, BLOCK, LANES), F32),
            pltpu.VMEM((KD, BLOCK, BLOCK), BF16),
            pltpu.VMEM((KC * 6 * TRACE, BLOCK), BF16),
            pltpu.VMEM((rows, LANES), jnp.int32),
            pltpu.VMEM((6, rows, LANES), jnp.int32),
            pltpu.VMEM((BLOCK, DEPTH), BF16),
            pltpu.VMEM((6 * TRACE, DEPTH), BF16),
            pltpu.VMEM((KC * LATERAL, 3 * LANES), BF16),
            pltpu.VMEM((BLOCK, KC * LATERAL), BF16),
            pltpu.VMEM((2, BLOCK, KC * TRACE), BF16),
            pltpu.VMEM((groups, KD, PACK, COLS), BF16),
            pltpu.VMEM((groups, 6, PACK, COLS), BF16),
            pltpu.VMEM((groups, BLOCK, COLS), F32),
            pltpu.VMEM((KC * LATERAL, COLS), BF16),
            pltpu.VMEM((KC * TRACE, COLS), BF16),
            pltpu.VMEM((groups, DEPTH, COLS), BF16),
            pltpu.VMEM((KD * KC * TRACE, COLS), BF16),
            pltpu.VMEM((groups, LATERAL + TRACE, COLS), F32),
            pltpu.VMEM((2, LATERAL, KD * KC * TRACE), BF16),
            pltpu.VMEM((2, TRACE, KD * KC * TRACE), BF16),
            pltpu.VMEM((BLOCK, KD * KC * TRACE), BF16),
            pltpu.VMEM((HALVES, groups, TRACE, COLS), BF16),
            pltpu.VMEM((HALVES, groups, TRACE, COLS), BF16),
            pltpu.VMEM((HALVES - 1, rows + 2, TRACE, LANES), BF16),
            pltpu.VMEM((HALVES - 1, rows + 2, TRACE, LANES), BF16),
            pltpu.VMEM((HALVES - 1, 2, rows, TRACE, LANES), BF16),
            pltpu.VMEM((HALVES - 1, 2, groups, TRACE, LANES), BF16),
            pltpu.VMEM((HALVES - 1, 2, groups, TRACE, LANES), BF16),
            pltpu.SemaphoreType.DMA((4 + rows,)),
            pltpu.SemaphoreType.DMA((HALVES, groups)),
            pltpu.SemaphoreType.DMA((HALVES, groups)),
            pltpu.SemaphoreType.DMA((HALVES - 1, 2)),
            pltpu.SemaphoreType.DMA((HALVES - 1, 2)),
            pltpu.SemaphoreType.DMA((HALVES - 1, 2, groups)),
            pltpu.SemaphoreType.DMA((HALVES - 1, 2, groups)),
        ],
        compiler_params=pltpu.CompilerParams(
            collective_id=0, has_side_effects=True, vmem_limit_bytes=48 << 20
        ),
    )(
        *[
            pltpu.with_memory_space_constraint(one, pltpu.HBM)
            for one in (
                right_side,
                inverse_table,
                coupling_table.reshape(KC * 6 * TRACE, BLOCK),
                block_kind.reshape(rows, width_y),
                face_kind.reshape(6, rows, width_y),
            )
        ]
    )
    return result.reshape(right_side.shape)


def solution(mesh):
    in_specs = (
        P("sweep", None, "cx", "cy"),
        P(),
        P(),
        P("sweep", "cx", "cy"),
        P("sweep", None, "cx", "cy"),
    )
    out_specs = P("sweep", None, "cx", "cy")
    return jax.shard_map(shards, mesh=mesh, in_specs=in_specs, out_specs=out_specs, check_vma=False)
```

```python
import functools
import jax
import jax.numpy as jnp
from jax import lax
from jax.experimental import pallas as pl
from jax.experimental.pallas import tpu as pltpu
from jax.sharding import PartitionSpec as P

NVAR = 5
NP = 4
BLOCK = 320
TRACE = 80
KD = 4
KC = 2
SWEEPS = 2
HALVES = 2 * SWEEPS
LANES = 128
WIDE = 256
REST = BLOCK - WIDE
GROUP = 2
COLS = GROUP * LANES
DEPTH = KD * BLOCK
LATERAL = 4 * TRACE
PACK = 16
MESH = pl.DeviceIdType.MESH
F32 = jnp.float32
BF16 = jnp.bfloat16


def kernel(
    rows,
    rhs_hbm,
    table_hbm,
    coupling_hbm,
    kind_hbm,
    face_hbm,
    out_ref,
    rhs_ref,
    table_ref,
    coupling_ref,
    kind_ref,
    face_ref,
    full_ref,
    trace_ref,
    tall_ref,
    lat_ref,
    chain_ref,
    kmask_ref,
    fmask_ref,
    prod_ref,
    lat_stack,
    chain_stack,
    inv_stack,
    front_stack,
    ubase_ref,
    g_lat,
    g_front,
    g_full,
    front_in,
    front_out,
    x_low,
    x_high,
    y_own,
    y_in,
    y_out,
    load_sem,
    front_send,
    front_recv,
    x_send,
    x_recv,
    y_send,
    y_recv,
):
    groups = rows // GROUP
    places = {}
    for name in ("sweep", "cx", "cy"):
        places[name] = (lax.axis_index(name), lax.axis_size(name))

    def has(name, step):
        spot, count = places[name]
        return spot < count - 1 if step > 0 else spot > 0

    def partner(name, step):
        return {name: places[name][0] + step}

    for half in range(HALVES - 1):
        x_high[half, 0] = jnp.zeros((TRACE, LANES), BF16)
        x_low[half, rows + 1] = jnp.zeros((TRACE, LANES), BF16)
    for side in range(2):

        @pl.when(jnp.logical_not(has("cy", 2 * side - 1)))
        def _():
            for half in range(HALVES - 1):
                y_in[half, side] = jnp.zeros((groups, TRACE, LANES), BF16)

    barrier = pltpu.get_barrier_semaphore()
    total = 0
    for name in ("sweep", "cx", "cy"):
        for step in (-1, 1):
            exists = has(name, step)
            total = total + jnp.where(exists, 1, 0)

            @pl.when(exists)
            def _():
                pl.semaphore_signal(
                    barrier, inc=1, device_id=partner(name, step), device_id_type=MESH
                )

    loads = [
        pltpu.make_async_copy(table_hbm, table_ref, load_sem.at[0]),
        pltpu.make_async_copy(kind_hbm, kind_ref, load_sem.at[1]),
        pltpu.make_async_copy(face_hbm, face_ref, load_sem.at[2]),
        pltpu.make_async_copy(coupling_hbm, coupling_ref, load_sem.at[3]),
    ]
    for row in range(rows):
        loads.append(
            pltpu.make_async_copy(rhs_hbm.at[0, :, row, :], rhs_ref.at[row], load_sem.at[4 + row])
        )
    for one in loads[:3] + loads[4:] + loads[3:4]:
        one.start()

    def picks(start, count):
        line = lax.broadcasted_iota(jnp.int32, (count, BLOCK), 0) + start
        spot = lax.broadcasted_iota(jnp.int32, (count, BLOCK), 1)
        block = line // TRACE
        inner = line - block * TRACE
        var = inner // (NP * NP)
        first = (inner // NP) % NP
        second = inner % NP
        last = NP - 1
        along = jnp.where(block == 0, last, 0) * NP * NP + first * NP + second
        cross_x = first * NP * NP + jnp.where(block == 2, last, 0) * NP + second
        cross_y = first * NP * NP + second * NP + jnp.where(block == 4, last, 0)
        is_x = jnp.logical_or(block == 1, block == 2)
        is_y = jnp.logical_or(block == 3, block == 4)
        feature = jnp.where(is_x, cross_x, jnp.where(is_y, cross_y, along))
        feature = feature + var * (NP * NP * NP)
        return jnp.where(spot == feature, 1.0, 0.0).astype(BF16)

    def pick_rows(chosen, start, count):
        for part in range(DEPTH // WIDE):
            lanes = slice(part * WIDE, (part + 1) * WIDE)
            trace_ref[start : start + count, lanes] = jnp.dot(
                chosen, full_ref[:, lanes], preferred_element_type=F32
            ).astype(BF16)

    some = picks(0, TRACE)
    loads[0].wait()
    for kind in range(KD):
        full_ref[:, kind * WIDE : (kind + 1) * WIDE] = table_ref[kind, :, :WIDE]
    for pair in range(KD // 2):
        full_ref[:, KD * WIDE + pair * LANES : KD * WIDE + (pair + 1) * LANES] = jnp.concatenate(
            [table_ref[2 * pair, :, WIDE:], table_ref[2 * pair + 1, :, WIDE:]], axis=1
        )
    pick_rows(some, 0, TRACE)

    loads[1].wait()
    loads[2].wait()
    for row in range(rows):
        group, lanes = row // GROUP, slice(row % GROUP * LANES, (row % GROUP + 1) * LANES)
        kinds = jnp.broadcast_to(kind_ref[row : row + 1, :], (PACK, LANES))
        for kind in range(KD):
            kmask_ref[group, kind, :, lanes] = jnp.where(kinds == kind, 1.0, 0.0).astype(BF16)
        for face in range(6):
            one = jnp.broadcast_to(face_ref[face, row : row + 1, :], (PACK, LANES))
            fmask_ref[group, face, :, lanes] = one.astype(F32).astype(BF16)

    def lay_out_coupling():
        loads[3].wait()
        for face in range(2):
            for kind in range(KC):
                tall_ref[kind * TRACE : (kind + 1) * TRACE, :BLOCK] = coupling_ref[
                    (kind * 6 + face) * TRACE : (kind * 6 + face + 1) * TRACE, :
                ]
            chain_ref[face] = jnp.transpose(tall_ref[: 2 * LANES, :])[:BLOCK, : KC * TRACE]
        for kind in range(KC):
            tall_ref[kind * LATERAL : (kind + 1) * LATERAL, :BLOCK] = coupling_ref[
                (kind * 6 + 2) * TRACE : (kind * 6 + 6) * TRACE, :
            ]
        lat_ref[...] = jnp.transpose(tall_ref[...])[:BLOCK]

    def corrected(rows_ref, start, count, face, target):
        for kind in range(KD):
            low, rest = kind * WIDE, KD * WIDE + kind * REST
            value = jnp.dot(
                rows_ref[start : start + count, low : low + WIDE],
                chain_ref[face, :WIDE, :],
                preferred_element_type=F32,
            ) + jnp.dot(
                rows_ref[start : start + count, rest : rest + REST],
                chain_ref[face, WIDE:, :],
                preferred_element_type=F32,
            )
            target[:, kind * KC * TRACE : (kind + 1) * KC * TRACE] = value.astype(BF16)

    for row in range(rows):
        loads[4 + row].wait()
    pl.semaphore_wait(barrier, total)

    lane = lax.broadcasted_iota(jnp.int32, (TRACE, LANES), 1)
    edges = (jnp.where(lane == 0, 1.0, 0.0), jnp.where(lane == LANES - 1, 1.0, 0.0))
    flip = lax.rem(places["cx"][0], 2)

    def place_of(turn):
        group = jnp.where(turn == 0, 0, jnp.where(turn == 1, groups - 1, turn - 1))
        return group + flip * (groups - 1 - 2 * group)

    def front_copy(half, group, step):
        return pltpu.make_async_remote_copy(
            src_ref=front_out.at[half, group],
            dst_ref=front_in.at[half, group],
            send_sem=front_send.at[half, group],
            recv_sem=front_recv.at[half, group],
            device_id=partner("sweep", step),
            device_id_type=MESH,
        )

    def x_copy(half, side):
        source, target = (x_low.at[half, 1], x_low.at[half, rows + 1])
        if side == 1:
            source, target = (x_high.at[half, rows], x_high.at[half, 0])
        return pltpu.make_async_remote_copy(
            src_ref=source,
            dst_ref=target,
            send_sem=x_send.at[half, side],
            recv_sem=x_recv.at[half, 1 - side],
            device_id=partner("cx", 2 * side - 1),
            device_id_type=MESH,
        )

    def y_copy(half, side, group):
        return pltpu.make_async_remote_copy(
            src_ref=y_out.at[half, side, group],
            dst_ref=y_in.at[half, 1 - side, group],
            send_sem=y_send.at[half, side, group],
            recv_sem=y_recv.at[half, 1 - side, group],
            device_id=partner("cy", 2 * side - 1),
            device_id_type=MESH,
        )

    def x_here(side, group):
        return jnp.logical_and(has("cx", 2 * side - 1), group == (groups - 1) * side)

    def put_masked(stack, place, lanes, value, mask, apart):
        tiles = value.reshape(-1, PACK, value.shape[-1])
        one = tiles * mask[None]
        stack[place : place + TRACE, lanes] = (tiles - one).reshape(value.shape)
        stack[place + apart : place + apart + TRACE, lanes] = one.reshape(value.shape)

    def turned(value, shift):
        return pltpu.roll(value, shift % LANES, 1) if shift % LANES else value

    def lateral(half, group):
        for side in range(2):

            @pl.when(x_here(side, group))
            def _():
                x_copy(half, 1 - side).wait_recv()

            @pl.when(has("cy", 2 * side - 1))
            def _():
                y_copy(half, 1 - side, group).wait_recv()

        for local in range(GROUP):
            row = group * GROUP + local
            lanes = slice(local * LANES, (local + 1) * LANES)
            values = [x_high[half, row], x_low[half, row + 2]]
            for side in range(2):
                seen = turned(y_in[half, side, group].astype(F32), local * (2 * side - 1))
                own = y_own[half, side, row].astype(F32)
                values.append((own + seen * edges[side]).astype(BF16))
            for face in range(4):
                mask = fmask_ref[group, 2 + face, :, lanes]
                put_masked(lat_stack, face * TRACE, lanes, values[face], mask, LATERAL)
        return jnp.dot(lat_ref[...], lat_stack[...], preferred_element_type=F32)

    def product_of(half, group, face):
        put_masked(
            chain_stack, 0, slice(None), front_in[half, group], fmask_ref[group, face], TRACE
        )
        return jnp.dot(chain_ref[face], chain_stack[...], preferred_element_type=F32)

    def rhs_of(group):
        return jnp.concatenate([rhs_ref[group * GROUP + local] for local in range(GROUP)], axis=1)

    def spread(residual, group):
        tiles = residual.astype(BF16).reshape(BLOCK // PACK, PACK, COLS)
        for kind in range(KD):
            masked = (tiles * kmask_ref[group, kind][None]).reshape(BLOCK, COLS)
            rest = KD * WIDE + kind * REST
            inv_stack[group, kind * WIDE : (kind + 1) * WIDE, :] = masked[:WIDE]
            inv_stack[group, rest : rest + REST, :] = masked[WIDE:]

    def inverse_rows(rows_ref, start, count, group):
        return jnp.dot(
            rows_ref[start : start + count, :], inv_stack[group], preferred_element_type=F32
        )

    def spread_front(half, group, face):
        seen = front_in[half, group].reshape(TRACE // PACK, PACK, COLS)
        high = seen * fmask_ref[group, face][None]
        parts = (seen - high, high)
        for kind in range(KD):
            for which in range(KC):
                place = (kind * KC + which) * TRACE
                one = parts[which] * kmask_ref[group, kind][None]
                front_stack[place : place + TRACE, :] = one.reshape(TRACE, COLS)

    def correction(table):
        return jnp.dot(table, front_stack[...], preferred_element_type=F32)

    def put_out(group, value):
        for local in range(GROUP):
            row = group * GROUP + local
            out_ref[pl.ds(row, BLOCK, stride=rows), :] = value[
                :, local * LANES : (local + 1) * LANES
            ]

    def send_front(half, group, step, value):
        front_out[half, group] = value.astype(BF16)
        front_copy(half, group, step).start()

    def emit(half, group, value):
        for local in range(GROUP):
            row = group * GROUP + local
            lanes = slice(local * LANES, (local + 1) * LANES)
            x_low[half, row + 1] = value[:TRACE, lanes].astype(BF16)
            x_high[half, row + 1] = value[TRACE : 2 * TRACE, lanes].astype(BF16)
        for side in range(2):

            @pl.when(x_here(side, group))
            def _():
                x_copy(half, side).start()

        for side in range(2):
            start = (2 + side) * TRACE
            packed = jnp.zeros((TRACE, LANES), F32)
            away = 1 - 2 * (1 - side)
            edge = 1 - side
            for local in range(GROUP):
                row = group * GROUP + local
                one = value[start : start + TRACE, local * LANES : (local + 1) * LANES]
                moved = turned(one, away)
                y_own[half, edge, row] = (moved * (1.0 - edges[edge])).astype(BF16)
                spot = local if side == 1 else LANES - 1 - local
                packed = jnp.where(lane == spot, turned(one, away * (1 + local)), packed)
            y_out[half, side, group] = packed.astype(BF16)

            @pl.when(has("cy", 2 * side - 1))
            def _():
                y_copy(half, side, group).start()

    def each_group(body):
        @pl.loop(0, groups)
        def _(turn):
            body(place_of(turn))

    def set_up_rest():
        lay_out_coupling()
        pick_rows(picks(TRACE, 5 * TRACE), TRACE, 5 * TRACE)

        @pl.when(has("sweep", -1))
        def _():
            corrected(trace_ref, TRACE, LATERAL, 0, g_lat.at[0])

            @pl.when(has("sweep", 1))
            def _():
                corrected(trace_ref, 0, TRACE, 0, g_front.at[0])

    def set_up_back():
        @pl.when(has("sweep", 1))
        def _():
            corrected(trace_ref, TRACE, LATERAL, 1, g_lat.at[1])
            corrected(full_ref, 0, BLOCK, 1, g_full)

            @pl.when(has("sweep", -1))
            def _():
                corrected(trace_ref, 5 * TRACE, TRACE, 1, g_front.at[1])

    for half in range(HALVES):
        step = 1 if half % 2 == 0 else -1
        face = 0 if half % 2 == 0 else 1
        front_rows = 0 if half % 2 == 0 else 5 * TRACE
        final = half == HALVES - 1
        upstream = has("sweep", -step)
        downstream = has("sweep", step)

        def start_of(group):
            start = rhs_of(group)
            if half > 0:
                start = start - lateral(half - 1, group) - prod_ref[group]
            return start

        @pl.when(jnp.logical_not(upstream))
        def _():
            def first_part(group):
                spread(start_of(group), group)

                @pl.when(downstream)
                def _():
                    send_front(half, group, step, inverse_rows(trace_ref, front_rows, TRACE, group))

            each_group(first_part)

        if half == 0:
            set_up_rest()

        @pl.when(jnp.logical_not(upstream))
        def _():
            def second_part(group):
                if final:
                    put_out(group, inverse_rows(full_ref, 0, BLOCK, group))
                else:
                    emit(half, group, inverse_rows(trace_ref, TRACE, LATERAL, group))
                    prod_ref[group] = jnp.zeros((BLOCK, COLS), F32)

            each_group(second_part)

        if half == 0:
            set_up_back()

        @pl.when(upstream)
        def _():
            def before(group):
                spread(start_of(group), group)
                if final:
                    ubase_ref[group, :BLOCK] = inverse_rows(full_ref, 0, BLOCK, group)
                else:
                    ubase_ref[group, :LATERAL] = inverse_rows(trace_ref, TRACE, LATERAL, group)

                @pl.when(downstream)
                def _():
                    ubase_ref[group, LATERAL:] = inverse_rows(trace_ref, front_rows, TRACE, group)

            def arrived(group):
                front_copy(half, group, step).wait_recv()
                spread_front(half, group, face)

                @pl.when(downstream)
                def _():
                    send_front(
                        half, group, step, ubase_ref[group, LATERAL:] - correction(g_front[face])
                    )

                if final:
                    put_out(group, ubase_ref[group, :BLOCK] - correction(g_full[...]))
                else:
                    emit(half, group, ubase_ref[group, :LATERAL] - correction(g_lat[face]))

            def after(group):
                prod_ref[group] = product_of(half, group, face)

            each_group(before)
            each_group(arrived)
            if not final:
                each_group(after)

    for half in range(HALVES):
        step = 1 if half % 2 == 0 else -1

        @pl.when(has("sweep", step))
        def _():
            @pl.loop(0, groups)
            def _(group):
                front_copy(half, group, step).wait_send()

        if half < HALVES - 1:
            for side in range(2):

                @pl.when(has("cy", 2 * side - 1))
                def _():
                    @pl.loop(0, groups)
                    def _(group):
                        y_copy(half, side, group).wait_send()

                @pl.when(has("cx", 2 * side - 1))
                def _():
                    x_copy(half, side).wait_send()


def shards(right_side, inverse_table, coupling_table, block_kind, face_kind):
    _, _, rows, width_y = right_side.shape
    groups = rows // GROUP
    result = pl.pallas_call(
        functools.partial(kernel, rows),
        out_shape=jax.ShapeDtypeStruct((BLOCK * rows, LANES), F32),
        in_specs=[pl.BlockSpec(memory_space=pl.ANY)] * 5,
        out_specs=pl.BlockSpec(memory_space=pltpu.VMEM),
        scratch_shapes=[
            pltpu.VMEM((rows, BLOCK, LANES), F32),
            pltpu.VMEM((KD, BLOCK, BLOCK), BF16),
            pltpu.VMEM((KC * 6 * TRACE, BLOCK), BF16),
            pltpu.VMEM((rows, LANES), jnp.int32),
            pltpu.VMEM((6, rows, LANES), jnp.int32),
            pltpu.VMEM((BLOCK, DEPTH), BF16),
            pltpu.VMEM((6 * TRACE, DEPTH), BF16),
            pltpu.VMEM((KC * LATERAL, 3 * LANES), BF16),
            pltpu.VMEM((BLOCK, KC * LATERAL), BF16),
            pltpu.VMEM((2, BLOCK, KC * TRACE), BF16),
            pltpu.VMEM((groups, KD, PACK, COLS), BF16),
            pltpu.VMEM((groups, 6, PACK, COLS), BF16),
            pltpu.VMEM((groups, BLOCK, COLS), F32),
            pltpu.VMEM((KC * LATERAL, COLS), BF16),
            pltpu.VMEM((KC * TRACE, COLS), BF16),
            pltpu.VMEM((groups, DEPTH, COLS), BF16),
            pltpu.VMEM((KD * KC * TRACE, COLS), BF16),
            pltpu.VMEM((groups, LATERAL + TRACE, COLS), F32),
            pltpu.VMEM((2, LATERAL, KD * KC * TRACE), BF16),
            pltpu.VMEM((2, TRACE, KD * KC * TRACE), BF16),
            pltpu.VMEM((BLOCK, KD * KC * TRACE), BF16),
            pltpu.VMEM((HALVES, groups, TRACE, COLS), BF16),
            pltpu.VMEM((HALVES, groups, TRACE, COLS), BF16),
            pltpu.VMEM((HALVES - 1, rows + 2, TRACE, LANES), BF16),
            pltpu.VMEM((HALVES - 1, rows + 2, TRACE, LANES), BF16),
            pltpu.VMEM((HALVES - 1, 2, rows, TRACE, LANES), BF16),
            pltpu.VMEM((HALVES - 1, 2, groups, TRACE, LANES), BF16),
            pltpu.VMEM((HALVES - 1, 2, groups, TRACE, LANES), BF16),
            pltpu.SemaphoreType.DMA((4 + rows,)),
            pltpu.SemaphoreType.DMA((HALVES, groups)),
            pltpu.SemaphoreType.DMA((HALVES, groups)),
            pltpu.SemaphoreType.DMA((HALVES - 1, 2)),
            pltpu.SemaphoreType.DMA((HALVES - 1, 2)),
            pltpu.SemaphoreType.DMA((HALVES - 1, 2, groups)),
            pltpu.SemaphoreType.DMA((HALVES - 1, 2, groups)),
        ],
        compiler_params=pltpu.CompilerParams(
            collective_id=0, has_side_effects=True, vmem_limit_bytes=48 << 20
        ),
    )(
        *[
            pltpu.with_memory_space_constraint(one, pltpu.HBM)
            for one in (
                right_side,
                inverse_table,
                coupling_table.reshape(KC * 6 * TRACE, BLOCK),
                block_kind.reshape(rows, width_y),
                face_kind.reshape(6, rows, width_y),
            )
        ]
    )
    return result.reshape(right_side.shape)


def solution(mesh):
    in_specs = (
        P("sweep", None, "cx", "cy"),
        P(),
        P(),
        P("sweep", "cx", "cy"),
        P("sweep", None, "cx", "cy"),
    )
    out_specs = P("sweep", None, "cx", "cy")
    return jax.shard_map(shards, mesh=mesh, in_specs=in_specs, out_specs=out_specs, check_vma=False)
```
